32 devices in a mesh: span: 2 (over y), tmpl: 2 (over x), stn: 8 (over z, core).
Axes of the slice: x: 2, y: 2, z: 4, core: 2. Of those that a mesh axis runs over, the one named last changes fastest.
Arguments:
- signal: bfloat16 [3072, 8192], P('stn', ('span', 'tmpl')), parts along dimension 1, may hold values from -110 to 110
- waveforms: bfloat16 [16, 4, 8, 300], P('tmpl'), may hold values from -40 to 40
- station_groups: int32 [16, 4], P('tmpl'), may hold values from 0 to 7, all different within a row; in each aligned block of 8 rows (0 to 7, 8 to 15, ...) at most 8 rows name the same one
- channel_offsets: int32 [16, 4, 8], P('tmpl'), may hold values from 0 to 383
- moveouts: int32 [16, 4, 8], P('tmpl'), may hold values from 0 to 639
Outputs:
- stack: float32 [16, 6144], P(('tmpl', 'stn'), 'span'), parts along dimension 1
The draws below stay inside these ranges and needn't reach their ends.
There are 2 independent parts, one for each index of `span`. The reference program is written for one: setup_inputs(seed, part) draws one part's arguments, and reference() takes and returns one part's arrays. A program takes and returns all parts, laid end to end along the dimension named above; an argument that names none is the same for every part. Nothing has to cross between parts.
Inputs may be any that keep to these rules, and one draw needn't show every extreme that they name: `station_groups`: A template's 4 station groups are distinct. Among the 8 templates of one index of tmpl, at most 8 touch any one station group, and in every draw some station group is touched by exactly 8 of them.
All inputs are finite; a program needn't handle non-finite values.
Results may differ from the reference program's by a relative error of at most 0.0003.
Values may be sent and summed in bfloat16 or wider, within the bound.
No kernel may reach another device: no remote copies, remote signals or barrier semaphores. Data moves between devices by JAX's collectives and lax.ppermute only.
A program may use at most 64 MiB of HBM per device.

```python
import math
import jax
import jax.numpy as jnp
import numpy as np
from jax import lax

C = 3072
L = 300
SL = 8
TOUCH = 4
MV = 640
NT = 3072
TG = 8
K = 16
TCAP = 8
S = 4096
N_STN = 8


def draw_signal(key, part):
    key_scale, key_env, key_base = jax.random.split(key, 3)
    chan_scale = jnp.exp(jax.random.uniform(key_scale, (C, 1), minval=0.0, maxval=math.log(10.0)))
    envelope = jnp.exp(jax.random.uniform(key_env, (1, S // 128), minval=-0.7, maxval=0.7))
    envelope = jnp.repeat(envelope, 128, axis=1)
    base = jax.random.normal(key_base, (C, S))
    base = jnp.clip(base, -5.0, 5.0)
    return (base * chan_scale * envelope).astype(jnp.bfloat16)


def draw_waveforms(key, part):
    key_scale, key_base = jax.random.split(jax.random.fold_in(key, 7), 2)
    slot_scale = jnp.exp(jax.random.uniform(key_scale, (K, TOUCH, SL, 1), minval=0.0, maxval=math.log(10.0)))
    base = jnp.clip(jax.random.normal(key_base, (K, TOUCH, SL, L)), -4.0, 4.0)
    return (base * slot_scale).astype(jnp.bfloat16)


def place_ends(drawn, rng, low, high):
    shape = drawn.shape
    spot = [jax.random.randint(jax.random.fold_in(rng, axis), (), 0, shape[axis]) for axis in range(len(shape))]
    drawn = drawn.at[tuple(spot)].set(low)
    longest = shape.index(max(shape))
    spot[longest] = (spot[longest] + 1) % shape[longest]
    return drawn.at[tuple(spot)].set(high)


def shared_out(key, own, number, rows, amount, top, reach, skew):
    sequence = jax.random.permutation(key, amount)
    packed, usual = portions_of(amount, rows * top, reach, skew, True), portions_of(amount, rows * top, reach, skew, False)
    places = jnp.arange(amount)

    def named(sizes, offset_by):
        used = int((sizes > 0).sum())
        fixed = max(1, used // 4)
        moved = fixed + (places - fixed + offset_by * (used - fixed)) % max(1, amount - fixed)
        return jnp.zeros((amount,), jnp.int32).at[sequence[jnp.where(places < fixed, places, moved)]].set(jnp.asarray(sizes, jnp.int32))

    sizes = jnp.where(number % 4 == 0, named(packed, number // 4), named(usual, number - number // 4 - 1))
    mixed = jax.random.permutation(jax.random.fold_in(own, 3), amount)
    source_of, taker = mixed[0:amount // 2 * 2:2], mixed[1:amount // 2 * 2:2]
    slack = jnp.minimum(sizes[source_of] - 1, reach - sizes[taker]) // 2
    slack = jnp.where((source_of == sequence[0]) | (taker == sequence[0]) | (sizes[taker] == 0), 0, jnp.maximum(slack, 0))
    moved = jax.random.randint(jax.random.fold_in(own, 4), (amount // 2,), 0, 1 << 20) % (slack + 1)
    sizes = sizes.at[source_of].add(-moved).at[taker].add(moved)
    items = jnp.searchsorted(jnp.cumsum(sizes), jnp.arange(rows * top), side="right").astype(jnp.int32)
    listing = items.reshape(top, rows).T
    listing = listing[jax.random.permutation(jax.random.fold_in(own, 1), rows)]
    offset_by = jax.random.randint(jax.random.fold_in(own, 2), (rows, 1), 0, top)
    return jnp.take_along_axis(listing, (jnp.arange(top)[None, :] + offset_by) % top, axis=1)


def portions_of(amount, total, limit, slope, full):
    weights = [(1 << 20) // math.isqrt(rank ** slope) + 1 for rank in range(1, amount + 1)]
    largest = limit if full else min(limit, max(-(-total // amount), total * weights[0] // sum(weights)))
    least = 1 if total - largest >= amount - 1 else 0
    given, surplus = [largest] + [least] * (amount - 1), total - largest - least * (amount - 1)
    while surplus > 0:
        candidates = [i for i in range(1, amount) if given[i] < largest] or [i for i in range(1, amount) if given[i] < limit]
        mass, left = sum([weights[i] for i in candidates]), surplus
        for i in candidates:
            extra = min(limit - given[i], max(1, left * weights[i] // mass), surplus)
            given[i] = given[i] + extra
            surplus = surplus - extra
    return np.array(given)


def setup_inputs(seed: int = 0, part: int = 0) -> dict:
    seeds = jax.random.split(jax.random.key(seed), 6)
    own_keys = jax.random.split(jax.random.fold_in(seeds[5], part), 6)
    signal = draw_signal(jax.random.fold_in(jax.random.fold_in(seeds[5], part), 71), part)
    waveforms = draw_waveforms(jax.random.fold_in(seeds[5], 71), part)
    station_groups_keys = jax.random.split(jax.random.fold_in(seeds[2], 1), K // TG)
    station_groups_turns = jax.random.permutation(jax.random.fold_in(seeds[2], 3), K // TG)
    station_groups = jax.vmap(lambda own, number: shared_out(jax.random.fold_in(seeds[2], 2), own, number, TG, N_STN, TOUCH, TCAP, 2))(station_groups_keys, station_groups_turns).reshape((K, TOUCH))
    channel_offsets = place_ends(jax.random.randint(seeds[3], (K, TOUCH, SL), 0, C // N_STN), jax.random.fold_in(seeds[3], 1), 0, (C // N_STN) - 1).astype(jnp.int32)
    moveouts = place_ends(jax.random.randint(seeds[4], (K, TOUCH, SL), 0, MV), jax.random.fold_in(seeds[4], 1), 0, MV - 1).astype(jnp.int32)
    return {"signal": signal, "waveforms": waveforms, "station_groups": station_groups, "channel_offsets": channel_offsets, "moveouts": moveouts}


def reference(signal, waveforms, station_groups, channel_offsets, moveouts):
    data = signal.astype(jnp.float32)
    squares = data * data
    running = jnp.concatenate([jnp.zeros((C, 1), jnp.float32), jnp.cumsum(squares, axis=1)], axis=1)
    windows = running[:, L:] - running[:, :-L]
    rms_data = jnp.sqrt(windows / L + 1e-05)
    channel_of = (station_groups[:, :, None] * (C // N_STN) + channel_offsets).astype(jnp.int32)
    fft_len = NT + L

    def per_template(inputs):
        waves, chans, moves = inputs
        waves = waves.reshape(TOUCH * SL, L).astype(jnp.float32)
        chans = chans.reshape(TOUCH * SL)
        moves = moves.reshape(TOUCH * SL)

        def one_slot(channel, lag_shift):
            segment = lax.dynamic_slice(data, (channel, lag_shift), (1, NT + L - 1)).reshape(NT + L - 1)
            scale_row = lax.dynamic_slice(rms_data, (channel, lag_shift), (1, NT)).reshape(NT)
            return (segment, scale_row)
        segments, scales = jax.vmap(one_slot)(chans, moves)
        spectrum = jnp.fft.rfft(segments, n=fft_len) * jnp.conj(jnp.fft.rfft(waves, n=fft_len))
        correl = jnp.fft.irfft(spectrum, n=fft_len)[:, :NT]
        wave_rms = jnp.sqrt(lax.optimization_barrier(jnp.mean(waves * waves, axis=1)) + 1e-05)
        return lax.optimization_barrier(jnp.sum(correl / (L * wave_rms[:, None] * scales), axis=0))
    return lax.map(per_template, (waveforms, channel_of, moveouts))
```

```python
import functools
import jax
import jax.numpy as jnp
from jax import lax
from jax.experimental import pallas as pl
from jax.experimental.pallas import tpu as pltpu
from jax.sharding import PartitionSpec as P

NT = 3072
LANES = 128
eps_value = 1e-05
KERNEL_VMEM = 24 << 20


def touch_of(groups_ref, k):
    station = lax.axis_index("stn")
    touch = jnp.int32(0)
    for g in range(1, groups_ref.shape[0]):
        touch = jnp.where(groups_ref[g, k] == station, g, touch)
    return touch


def toeplitz_kernel(slots, length, span, groups_ref, waves_ref, tiles_ref, inv_ref):
    half = jnp.zeros((slots, span - waves_ref.shape[3]), jnp.float32)

    def one_template(k, carry):
        touch = touch_of(groups_ref, k)
        waves = waves_ref[k, touch].astype(jnp.float32)
        power = jnp.sum(waves * waves, axis=1, keepdims=True) / length
        inv = 1.0 / (length * jnp.sqrt(power + eps_value))
        inv_ref[pl.ds(k * slots, slots), :] = jnp.broadcast_to(inv, (slots, LANES))
        padded = jnp.concatenate([waves, half], axis=1)
        for s in range(slots):
            row = jnp.broadcast_to(padded[s : s + 1, :], (LANES, span))
            rolled = pltpu.roll(row, 0, 1, stride=1, stride_axis=0)
            tiles_ref[k * slots + s] = rolled.astype(jnp.bfloat16)
        return carry

    lax.fori_loop(0, waves_ref.shape[0], one_template, 0)


def make_tiles(groups, waves):
    rows, _, slots, length = waves.shape
    span = LANES * (-(-(LANES + length - 1) // LANES))
    return pl.pallas_call(
        functools.partial(toeplitz_kernel, slots, length, span),
        out_shape=(
            jax.ShapeDtypeStruct((rows * slots, LANES, span), jnp.bfloat16),
            jax.ShapeDtypeStruct((rows * slots, LANES), jnp.float32),
        ),
        in_specs=[
            pl.BlockSpec(memory_space=pltpu.SMEM),
            pl.BlockSpec(memory_space=pltpu.VMEM),
        ],
        out_specs=(
            pl.BlockSpec(memory_space=pltpu.VMEM),
            pl.BlockSpec(memory_space=pltpu.VMEM),
        ),
        name="toeplitz",
        cost_estimate=pl.CostEstimate(flops=10000000, bytes_accessed=9000000, transcendentals=0),
        compiler_params=pltpu.CompilerParams(vmem_limit_bytes=KERNEL_VMEM),
    )(groups, waves)


def stack_kernel(slots, length, blocks, pieces, groups_ref, shift_ref, *refs):
    piece_refs, (tiles_ref, inv_ref, band_ref, out_ref, raw, rolled, aligned, sums) = refs[:pieces], refs[pieces:]
    rows = tiles_ref.shape[0]
    taps = tiles_ref.shape[2] // LANES
    pitch = raw.shape[0] // rows
    wide = aligned.shape[0] // slots
    raw[...] = jnp.zeros_like(raw)
    rolled[...] = jnp.zeros_like(rolled)
    for i, piece in enumerate(piece_refs):
        start = 0
        if pieces == 2:
            me = lax.axis_index("tmpl")
            start = (me if i == 0 else 1 - me) * (piece.shape[1] // LANES)
        for a in range(piece.shape[1] // LANES):
            for r in range(0, rows, 8):
                part = piece[r : r + 8, a * LANES : (a + 1) * LANES].astype(jnp.float32)
                raw[pl.ds(r * pitch + start + a, 8, stride=pitch), :] = part
    lane = lax.broadcasted_iota(jnp.int32, (wide, LANES), 1)

    def one_template(k, carry):
        touch = touch_of(groups_ref, k)
        for s in range(slots):
            shift = shift_ref[k, touch, s]
            whole = shift // LANES
            fine = shift - whole * LANES
            base = (k * slots + s) * pitch + whole
            turned = pltpu.roll(raw[pl.ds(base, wide), :], LANES - fine, 1)
            rolled[s, 0:wide, :] = turned
            value = jnp.where(lane < LANES - fine, turned, rolled[s, pl.ds(1, wide), :])
            aligned[s * wide : (s + 1) * wide, :] = value
        value = aligned[...]
        square = value * value
        high = square.astype(jnp.bfloat16)
        low = (square - high.astype(jnp.float32)).astype(jnp.bfloat16)
        sums[...] = jnp.dot(
            jnp.concatenate([high, low], axis=1), band_ref[...], preferred_element_type=jnp.float32
        )
        total = jnp.zeros((blocks, LANES), jnp.float32)
        for s in range(slots):
            row = k * slots + s
            window = jnp.concatenate(
                [aligned[pl.ds(s * wide + o, blocks), :] for o in range(taps)], axis=1
            ).astype(jnp.bfloat16)
            correl = lax.dot_general(
                window, tiles_ref[row], (((1,), (1,)), ((), ())), preferred_element_type=jnp.float32
            )
            energy = sums[pl.ds(s * wide, blocks), 0:LANES]
            for o in range(1, taps):
                energy = energy + sums[pl.ds(s * wide + o, blocks), o * LANES : (o + 1) * LANES]
            scale = lax.rsqrt(energy / length + eps_value) * inv_ref[pl.ds(row, 1), :]
            total = total + correl * scale
        out_ref[k] = total
        return carry

    lax.fori_loop(0, out_ref.shape[0], one_template, 0)


def make_stacks(groups, shifts, pieces, tiles, inv, band, templates, length, moveout_blocks):
    rows, _, span = tiles.shape
    slots = rows // templates
    blocks = NT // LANES
    wide = 8 * (-(-(blocks + span // LANES - 1) // 8))
    depth = sum(p.shape[1] for p in pieces) // LANES
    pitch = 8 * (-(-max(depth, wide + moveout_blocks) // 8))
    vmem = pl.BlockSpec(memory_space=pltpu.VMEM)
    smem = pl.BlockSpec(memory_space=pltpu.SMEM)
    return pl.pallas_call(
        functools.partial(stack_kernel, slots, length, blocks, len(pieces)),
        out_shape=jax.ShapeDtypeStruct((templates, blocks, LANES), jnp.float32),
        in_specs=[smem, smem] + [vmem] * (len(pieces) + 3),
        out_specs=vmem,
        scratch_shapes=[
            pltpu.VMEM((rows * pitch, LANES), jnp.float32),
            pltpu.VMEM((slots, wide + 8, LANES), jnp.float32),
            pltpu.VMEM((slots * wide, LANES), jnp.float32),
            pltpu.VMEM((slots * wide, span), jnp.float32),
        ],
        name="stack",
        cost_estimate=pl.CostEstimate(flops=400000000, bytes_accessed=9000000, transcendentals=0),
        compiler_params=pltpu.CompilerParams(vmem_limit_bytes=KERNEL_VMEM),
    )(groups, shifts, *pieces, tiles, inv, band)


def band_matrix(length, span):
    taps = span // LANES
    c = lax.broadcasted_iota(jnp.int32, (LANES, taps, LANES), 0)
    o = lax.broadcasted_iota(jnp.int32, (LANES, taps, LANES), 1)
    b = lax.broadcasted_iota(jnp.int32, (LANES, taps, LANES), 2)
    lag = LANES * o + c - b
    one = ((lag >= 0) & (lag < length)).astype(jnp.bfloat16).reshape(LANES, span)
    return jnp.concatenate([one, one], axis=0)


def pick_rows(groups, offsets, station, signal):
    count = signal.shape[0]
    here = (groups == station)[:, :, None, None]
    place = lax.broadcasted_iota(jnp.int32, (1, 1, 1, count), 3)
    hot = jnp.any(here & (offsets[..., None] == place), axis=1)
    hot = hot.reshape(-1, count).astype(signal.dtype)
    return jnp.dot(hot, signal, preferred_element_type=jnp.float32).astype(signal.dtype)


def sum_to_owner(stacks):
    stations = stacks.shape[0]
    if stations & (stations - 1):
        got = lax.all_to_all(stacks, "stn", split_axis=0, concat_axis=0, tiled=True)
        return jnp.sum(got, axis=0)
    me = lax.axis_index("stn")
    step = 1
    while step < stations:
        pairs = stacks.reshape((-1, 2) + stacks.shape[1:])
        bit = (me // step) % 2
        kept = lax.dynamic_index_in_dim(pairs, bit, 1, False)
        sent = lax.dynamic_index_in_dim(pairs, 1 - bit, 1, False)
        stacks = kept + lax.ppermute(sent, "stn", [(j, j ^ step) for j in range(stations)])
        step *= 2
    return stacks[0]


def shards(signal, waveforms, station_groups, channel_offsets, moveouts):
    templates, touches, slots, length = waveforms.shape
    count, samples = signal.shape
    parts = lax.axis_size("tmpl")
    stations = lax.axis_size("stn")
    station = lax.axis_index("stn")
    groups = station_groups.T
    if parts == 2:
        swap = [(0, 1), (1, 0)]
        asked = lax.ppermute(station_groups, "tmpl", swap), lax.ppermute(channel_offsets, "tmpl", swap)
        own = pick_rows(station_groups, channel_offsets, station, signal)
        sent = pick_rows(*asked, station, signal)
        sent, groups, own = lax.optimization_barrier((sent, groups, own))
        got = lax.ppermute(sent, "tmpl", swap)
        pieces = (own, got)
    else:
        asked = [lax.all_gather(x, "tmpl", axis=0, tiled=True) for x in (station_groups, channel_offsets)]
        sent = pick_rows(*asked, station, signal).reshape(parts, templates * slots, samples)
        got = lax.all_to_all(sent, "tmpl", split_axis=0, concat_axis=0, tiled=True)
        pieces = (got.transpose(1, 0, 2).reshape(templates * slots, parts * samples),)
    tiles, inv = make_tiles(groups, waveforms)
    band = band_matrix(length, tiles.shape[2])
    moveout_blocks = (parts * samples - NT - length) // LANES
    stacks = make_stacks(groups, moveouts, pieces, tiles, inv, band, templates, length, moveout_blocks)
    own_rows = templates // stations
    total = sum_to_owner(stacks.reshape((stations, own_rows) + stacks.shape[1:]))
    return total.reshape(own_rows, NT)


def solution(mesh):
    in_specs = (
        P("stn", ("span", "tmpl")),
        P("tmpl", None, None, None),
        P("tmpl", None),
        P("tmpl", None, None),
        P("tmpl", None, None),
    )
    out_specs = P(("tmpl", "stn"), "span")
    return jax.shard_map(shards, mesh=mesh, in_specs=in_specs, out_specs=out_specs, check_vma=False)
```

```python
import functools
import jax
import jax.numpy as jnp
from jax import lax
from jax.experimental import pallas as pl
from jax.experimental.pallas import tpu as pltpu
from jax.sharding import PartitionSpec as P

NT = 3072
LANES = 128
eps_value = 1e-05
KERNEL_VMEM = 24 << 20


def order_of(stations):
    bits = stations.bit_length() - 1
    reverse = lambda m: sum(((m >> b) & 1) << (bits - 1 - b) for b in range(bits))
    return sorted(range(stations), key=reverse, reverse=True)


def template_at(position, stations, templates, station):
    own_rows = templates // stations
    entry = order_of(stations)[position // own_rows]
    return (entry ^ station) * own_rows + position % own_rows


def touch_of(groups_ref, k, station):
    touch = jnp.int32(0)
    for g in range(1, groups_ref.shape[0]):
        touch = jnp.where(groups_ref[g, k] == station, g, touch)
    return touch


def toeplitz_kernel(slots, length, span, stations, groups_ref, waves_ref, tiles_ref, inv_ref):
    templates = waves_ref.shape[0]
    station = lax.axis_index("stn")
    tail = jnp.zeros((slots, span - length), jnp.float32)
    for p in range(templates):
        k = template_at(p, stations, templates, station)
        waves = waves_ref[k, touch_of(groups_ref, k, station)].astype(jnp.float32)
        power = jnp.sum(waves * waves, axis=1, keepdims=True) / length
        inv = 1.0 / (length * jnp.sqrt(power + eps_value))
        inv_ref[p * slots : (p + 1) * slots, :] = jnp.broadcast_to(inv, (slots, LANES))
        padded = jnp.concatenate([waves, tail], axis=1)
        for s in range(slots):
            row = jnp.broadcast_to(padded[s : s + 1, :], (LANES, span))
            rolled = pltpu.roll(row, 0, 1, stride=1, stride_axis=0)
            tiles_ref[p * slots + s] = rolled.astype(jnp.bfloat16)


def make_tiles(groups, waves, stations):
    templates, _, slots, length = waves.shape
    span = LANES * (-(-(LANES + length - 1) // LANES))
    vmem = pl.BlockSpec(memory_space=pltpu.VMEM)
    return pl.pallas_call(
        functools.partial(toeplitz_kernel, slots, length, span, stations),
        out_shape=(
            jax.ShapeDtypeStruct((templates * slots, LANES, span), jnp.bfloat16),
            jax.ShapeDtypeStruct((templates * slots, LANES), jnp.float32),
        ),
        in_specs=[pl.BlockSpec(memory_space=pltpu.SMEM), vmem],
        out_specs=(vmem, vmem),
        name="toeplitz",
        cost_estimate=pl.CostEstimate(flops=10000000, bytes_accessed=9000000, transcendentals=0),
        compiler_params=pltpu.CompilerParams(vmem_limit_bytes=KERNEL_VMEM),
    )(groups, waves)


def stack_kernel(slots, length, blocks, stations, positions, starts, groups_ref, shift_ref, *refs):
    pieces = len(starts)
    piece_refs, (tiles_ref, inv_ref, band_ref, out_ref, raw, rolled, aligned, sums) = refs[:pieces], refs[pieces:]
    templates = tiles_ref.shape[0] // slots
    taps = tiles_ref.shape[2] // LANES
    rows = len(positions) * slots
    pitch = raw.shape[0] // rows
    wide = aligned.shape[0] // rows
    station = lax.axis_index("stn")
    for i, piece in enumerate(piece_refs):
        start = 0
        if pieces == 2:
            me = lax.axis_index("tmpl")
            start = (me if i == 0 else 1 - me) * (piece.shape[1] // LANES)
        for a in range(piece.shape[1] // LANES):
            for r in range(0, rows, 8):
                first = starts[i] + r
                part = piece[first : first + 8, a * LANES : (a + 1) * LANES].astype(jnp.float32)
                raw[pl.ds(r * pitch + start + a, 8, stride=pitch), :] = part
    lane = lax.broadcasted_iota(jnp.int32, (wide, LANES), 1)

    def align(i):
        k = template_at(positions[i], stations, templates, station)
        touch = touch_of(groups_ref, k, station)
        for s in range(slots):
            row = i * slots + s
            shift = shift_ref[k, touch, s]
            whole = shift >> 7
            fine = shift & (LANES - 1)
            turned = pltpu.roll(raw[pl.ds(row * pitch + whole, wide), :], LANES - fine, 1)
            rolled[row, 0:wide, :] = turned
            value = jnp.where(lane < LANES - fine, turned, rolled[row, pl.ds(1, wide), :])
            aligned[row * wide : (row + 1) * wide, :] = value
        span = pl.ds(i * slots * wide, slots * wide)
        value = aligned[span, :]
        square = value * value
        high = square.astype(jnp.bfloat16)
        low = (square - high.astype(jnp.float32)).astype(jnp.bfloat16)
        sums[span, :] = jnp.dot(
            jnp.concatenate([high, low], axis=1), band_ref[...], preferred_element_type=jnp.float32
        )

    def stack(i):
        total = jnp.zeros((blocks, LANES), jnp.float32)
        for s in range(slots):
            row = positions[i] * slots + s
            first = (i * slots + s) * wide
            window = jnp.concatenate(
                [aligned[pl.ds(first + o, blocks), :] for o in range(taps)], axis=1
            ).astype(jnp.bfloat16)
            correl = lax.dot_general(
                window, tiles_ref[row], (((1,), (1,)), ((), ())), preferred_element_type=jnp.float32
            )
            energy = sums[pl.ds(first, blocks), 0:LANES]
            for o in range(1, taps):
                energy = energy + sums[pl.ds(first + o, blocks), o * LANES : (o + 1) * LANES]
            scale = lax.rsqrt(energy / length + eps_value) * inv_ref[pl.ds(row, 1), :]
            total = total + correl * scale
        out_ref[i] = total

    for i in range(len(positions)):
        align(i)
        if i:
            stack(i - 1)
    stack(len(positions) - 1)


def make_stacks(positions, groups, shifts, pieces, tiles, inv, band, length, stations):
    templates, _, slots = shifts.shape
    span = tiles.shape[2]
    rows = len(positions) * slots
    blocks = NT // LANES
    wide = 8 * (-(-(blocks + span // LANES - 1) // 8))
    depth = sum(p.shape[1] for p, _ in pieces) // LANES
    pitch = 8 * (-(-(depth + wide - blocks) // 8))
    vmem = pl.BlockSpec(memory_space=pltpu.VMEM)
    smem = pl.BlockSpec(memory_space=pltpu.SMEM)
    return pl.pallas_call(
        functools.partial(
            stack_kernel, slots, length, blocks, stations, positions, tuple(first for _, first in pieces)
        ),
        out_shape=jax.ShapeDtypeStruct((len(positions), blocks, LANES), jnp.float32),
        in_specs=[smem, smem] + [vmem] * (len(pieces) + 3),
        out_specs=vmem,
        scratch_shapes=[
            pltpu.VMEM((rows * pitch, LANES), jnp.float32),
            pltpu.VMEM((rows, wide + 8, LANES), jnp.float32),
            pltpu.VMEM((rows * wide, LANES), jnp.float32),
            pltpu.VMEM((rows * wide, span), jnp.float32),
        ],
        name="stack",
        cost_estimate=pl.CostEstimate(
            flops=50000000 * len(positions), bytes_accessed=1000000 * len(positions), transcendentals=0
        ),
        compiler_params=pltpu.CompilerParams(vmem_limit_bytes=KERNEL_VMEM),
    )(groups, shifts, *[p for p, _ in pieces], tiles, inv, band)


def band_matrix(length, span):
    taps = span // LANES
    c = lax.broadcasted_iota(jnp.int32, (LANES, taps, LANES), 0)
    o = lax.broadcasted_iota(jnp.int32, (LANES, taps, LANES), 1)
    b = lax.broadcasted_iota(jnp.int32, (LANES, taps, LANES), 2)
    lag = LANES * o + c - b
    one = ((lag >= 0) & (lag < length)).astype(jnp.bfloat16).reshape(LANES, span)
    return jnp.concatenate([one, one], axis=0)


def pick_rows(groups, offsets, station, stations, signal):
    templates, _, slots = offsets.shape
    count = signal.shape[0]
    named = jnp.stack([template_at(p, stations, templates, station) for p in range(templates)])
    here = (groups == station)[None] & (lax.iota(jnp.int32, templates)[None] == named[:, None])[:, :, None]
    wanted = jnp.sum(jnp.where(here[..., None], offsets[None] + 1, 0), axis=(1, 2)) - 1
    hot = wanted[..., None] == lax.broadcasted_iota(jnp.int32, (1, 1, count), 2)
    hot = hot.reshape(templates * slots, count).astype(signal.dtype)
    return jnp.dot(hot, signal, preferred_element_type=jnp.float32).astype(signal.dtype)


def shards(signal, waveforms, station_groups, channel_offsets, moveouts):
    templates, touches, slots, length = waveforms.shape
    samples = signal.shape[1]
    parts = lax.axis_size("tmpl")
    stations = lax.axis_size("stn")
    station = lax.axis_index("stn")
    groups = station_groups.T
    half, quarter = templates // 2, templates // 4
    if parts == 2:
        swap = [(0, 1), (1, 0)]
        if templates == slots:
            packed = lax.optimization_barrier(jnp.concatenate([channel_offsets, groups[None]], axis=0))
            named, asked = [(x[templates].T, x[:templates]) for x in (packed, lax.ppermute(packed, "tmpl", swap))]
        else:
            named = station_groups, channel_offsets
            asked = [lax.ppermute(x, "tmpl", swap) for x in named]
        own = pick_rows(*named, station, stations, signal)
        asked, own = lax.optimization_barrier((asked, own))
        sent = pick_rows(*asked, station, stations, signal)
        sent = sent[: half * slots], sent[half * slots :]
        sent, groups = lax.optimization_barrier((sent, groups))
        early = lax.ppermute(sent[0], "tmpl", swap)

        def pieces(first):
            return (own, first * slots), (got[first >= half], first % half * slots)
    else:
        asked = [lax.all_gather(x, "tmpl", axis=0) for x in (station_groups, channel_offsets)]
        sent = jnp.stack([pick_rows(asked[0][i], asked[1][i], station, stations, signal) for i in range(parts)])
        got = lax.all_to_all(sent, "tmpl", split_axis=0, concat_axis=0, tiled=True)
        got = got.transpose(1, 0, 2).reshape(templates * slots, parts * samples)

        def pieces(first):
            return ((got, first * slots),)

    tiles, inv = make_tiles(groups, waveforms, stations)
    if parts == 2:
        late, inv = lax.optimization_barrier((sent[1], inv))
        got = early, lax.ppermute(late, "tmpl", swap)
    band = band_matrix(length, tiles.shape[2])

    def stacks(first, last):
        positions = tuple(range(first, last))
        return make_stacks(positions, groups, moveouts, pieces(first), tiles, inv, band, length, stations)

    def across(x, step):
        return lax.ppermute(x, "stn", [(j, j ^ step) for j in range(stations)])

    came = across(stacks(0, half), 1)
    left = stacks(half, half + quarter) + came[:quarter]
    came_left = across(left, 2)
    total = stacks(half + quarter, templates) + came[quarter:] + came_left
    step = 4
    while step < stations:
        middle = total.shape[0] // 2
        total = total[middle:] + across(total[:middle], step)
        step *= 2
    return total.reshape(templates // stations, NT)


def solution(mesh):
    in_specs = (
        P("stn", ("span", "tmpl")),
        P("tmpl", None, None, None),
        P("tmpl", None),
        P("tmpl", None, None),
        P("tmpl", None, None),
    )
    out_specs = P(("tmpl", "stn"), "span")
    return jax.shard_map(shards, mesh=mesh, in_specs=in_specs, out_specs=out_specs, check_vma=False)
```

```python
import functools
import jax
import jax.numpy as jnp
from jax import lax
from jax.experimental import pallas as pl
from jax.experimental.pallas import tpu as pltpu
from jax.sharding import PartitionSpec as P

NT = 3072
LANES = 128
eps_value = 1e-05
KERNEL_VMEM = 24 << 20


def order_of(stations):
    bits = stations.bit_length() - 1
    reverse = lambda m: sum(((m >> b) & 1) << (bits - 1 - b) for b in range(bits))
    return sorted(range(stations), key=reverse, reverse=True)


def template_at(position, stations, templates, station):
    own_rows = templates // stations
    entry = order_of(stations)[position // own_rows]
    return (entry ^ station) * own_rows + position % own_rows


def toeplitz_kernel(
    slots, length, span, stations, groups_ref, shift_ref, waves_ref, tiles_ref, inv_ref, scalar_ref, padded, flipped
):
    templates = waves_ref.shape[0]
    taps = span // LANES
    rows = templates * slots
    station = lax.axis_index("stn")
    padded[...] = jnp.zeros_like(padded)
    groups = groups_ref[...]
    number = lax.broadcasted_iota(jnp.int32, groups.shape, 0)
    column = lax.broadcasted_iota(jnp.int32, groups.shape, 1)
    for p in range(templates):
        k = template_at(p, stations, templates, station)
        touch = jnp.sum(jnp.where((column == k) & (groups == station), number, 0))
        scalar_ref[p : p + 1, :] = shift_ref[k, pl.ds(touch, 1), :]
        waves = waves_ref[k, touch].astype(jnp.float32)
        power = jnp.sum(waves * waves, axis=1, keepdims=True) / length
        inv = 1.0 / (length * jnp.sqrt(power + eps_value))
        inv_ref[p * slots : (p + 1) * slots, :] = jnp.broadcast_to(inv, (slots, LANES))
        padded[p * slots : (p + 1) * slots, 0:length] = waves
    down = lax.broadcasted_iota(jnp.int32, (LANES, LANES), 0)
    along = lax.broadcasted_iota(jnp.int32, (LANES, LANES), 1)
    exchange = (down + along == LANES - 1).astype(jnp.bfloat16)
    for q in range(taps):
        block = padded[:, (taps - 1 - q) * LANES : (taps - q) * LANES].astype(jnp.bfloat16)
        flipped[:, q * LANES : (q + 1) * LANES] = jnp.dot(block, exchange, preferred_element_type=jnp.float32)
    for row in range(rows):
        turned = jnp.broadcast_to(flipped[row : row + 1, :], (LANES, span))
        turned = pltpu.roll(turned, 1, 1, stride=1, stride_axis=0).astype(jnp.bfloat16)
        for o in range(taps):
            lanes = (taps - o) % taps * LANES
            tiles_ref[row, o * LANES : (o + 1) * LANES, :] = turned[:, lanes : lanes + LANES]


def make_tiles(groups, shifts, waves, stations):
    templates, _, slots, length = waves.shape
    span = LANES * (-(-(LANES + length - 1) // LANES))
    rows = templates * slots
    vmem = pl.BlockSpec(memory_space=pltpu.VMEM)
    return pl.pallas_call(
        functools.partial(toeplitz_kernel, slots, length, span, stations),
        out_shape=(
            jax.ShapeDtypeStruct((rows, span, LANES), jnp.bfloat16),
            jax.ShapeDtypeStruct((rows, LANES), jnp.float32),
            jax.ShapeDtypeStruct((templates, slots), jnp.int32),
        ),
        in_specs=[vmem] * 3,
        out_specs=(vmem, vmem, vmem),
        scratch_shapes=[pltpu.VMEM((rows, span), jnp.float32), pltpu.VMEM((rows, span), jnp.float32)],
        name="toeplitz",
        cost_estimate=pl.CostEstimate(flops=10000000, bytes_accessed=9000000, transcendentals=0),
        compiler_params=pltpu.CompilerParams(vmem_limit_bytes=KERNEL_VMEM),
    )(groups, shifts, waves)


def stack_kernel(slots, length, blocks, positions, starts, scalar_ref, *refs):
    pieces = len(starts)
    piece_refs, refs = refs[:pieces], refs[pieces:]
    tiles_ref, inv_ref, band_ref, out_ref, raw, rolled, aligned, sums, whole = refs
    taps = tiles_ref.shape[1] // LANES
    rows = len(positions) * slots
    pitch = raw.shape[0] // rows
    wide = aligned.shape[0] // rows
    for i, piece in enumerate(piece_refs):
        start = 0
        if pieces == 2:
            me = lax.axis_index("tmpl")
            start = (me if i == 0 else 1 - me) * (piece.shape[1] // LANES)
        for a in range(piece.shape[1] // LANES):
            for r in range(0, rows, 8):
                first = starts[i] + r
                part = piece[first : first + 8, a * LANES : (a + 1) * LANES].astype(jnp.float32)
                raw[pl.ds(r * pitch + start + a, 8, stride=pitch), :] = part
    lane = lax.broadcasted_iota(jnp.int32, (wide, LANES), 1)

    scalars = scalar_ref[...]
    for i, position in enumerate(positions):
        for s in range(slots):
            row = i * slots + s
            shift = scalars[position, s]
            block = shift >> 7
            fine = shift & (LANES - 1)
            turned = pltpu.roll(raw[pl.ds(row * pitch + block, wide), :], LANES - fine, 1)
            rolled[row, 0:wide, :] = turned
            value = jnp.where(lane < LANES - fine, turned, rolled[row, pl.ds(1, wide), :])
            aligned[row * wide : (row + 1) * wide, :] = value
    value = aligned[...]
    square = value * value
    high = square.astype(jnp.bfloat16)
    low = (square - high.astype(jnp.float32)).astype(jnp.bfloat16)
    part = jnp.dot(jnp.concatenate([high, low], axis=1), band_ref[...], preferred_element_type=jnp.float32)
    sums[...] = part
    whole[...] = jnp.broadcast_to(part[:, 0:1], whole.shape)

    full, rest = length // LANES, length % LANES
    ahead = lax.broadcasted_iota(jnp.int32, (blocks, LANES), 1) < LANES - rest

    def energy_of(row):
        first = row * wide
        energy = sums[pl.ds(first, blocks), 0:LANES]
        for o in range(1, full):
            energy = energy + whole[pl.ds(first + o, blocks), :]
        near = sums[pl.ds(first + full, blocks), LANES : 2 * LANES]
        far = sums[pl.ds(first + full + 1, blocks), LANES : 2 * LANES]
        return energy + jnp.where(ahead, near, whole[pl.ds(first + full, blocks), :] + far)

    for i, position in enumerate(positions):
        total = jnp.zeros((blocks, LANES), jnp.float32)
        for s in range(0, slots, 2):
            row = i * slots + s
            window = jnp.concatenate(
                [
                    jnp.concatenate([aligned[pl.ds((row + h) * wide + o, blocks), :] for h in range(2)], axis=0)
                    for o in range(taps)
                ],
                axis=1,
            ).astype(jnp.bfloat16)
            first = position * slots + s
            tiles = jnp.concatenate([tiles_ref[first], tiles_ref[first + 1]], axis=1)
            correl = jnp.dot(window, tiles, preferred_element_type=jnp.float32)
            for h in range(2):
                weight = inv_ref[pl.ds(first + h, 1), :]
                scale = lax.rsqrt(energy_of(row + h) / length + eps_value) * weight
                total = total + correl[h * blocks : (h + 1) * blocks, h * LANES : (h + 1) * LANES] * scale
        out_ref[i] = total


def make_stacks(positions, scalars, slots, pieces, tiles, inv, band, length):
    taps = tiles.shape[1] // LANES
    rows = len(positions) * slots
    blocks = NT // LANES
    wide = 8 * (-(-(blocks + taps - 1) // 8))
    depth = sum(p.shape[1] for p, _ in pieces) // LANES
    pitch = 8 * (-(-(depth + wide - blocks) // 8))
    vmem = pl.BlockSpec(memory_space=pltpu.VMEM)
    return pl.pallas_call(
        functools.partial(stack_kernel, slots, length, blocks, positions, tuple(first for _, first in pieces)),
        out_shape=jax.ShapeDtypeStruct((len(positions), blocks, LANES), jnp.float32),
        in_specs=[vmem] * (len(pieces) + 4),
        out_specs=vmem,
        scratch_shapes=[
            pltpu.VMEM((rows * pitch, LANES), jnp.float32),
            pltpu.VMEM((rows, wide + 8, LANES), jnp.float32),
            pltpu.VMEM((rows * wide, LANES), jnp.float32),
            pltpu.VMEM((rows * wide, 2 * LANES), jnp.float32),
            pltpu.VMEM((rows * wide, LANES), jnp.float32),
        ],
        name="stack",
        cost_estimate=pl.CostEstimate(
            flops=50000000 * len(positions), bytes_accessed=1000000 * len(positions), transcendentals=0
        ),
        compiler_params=pltpu.CompilerParams(vmem_limit_bytes=KERNEL_VMEM),
    )(scalars, *[p for p, _ in pieces], tiles, inv, band)


def band_matrix(length):
    c = lax.broadcasted_iota(jnp.int32, (2 * LANES, 2 * LANES), 0) % LANES
    b = lax.broadcasted_iota(jnp.int32, (2 * LANES, 2 * LANES), 1)
    return jnp.where(b < LANES, c >= b, c < (b + length) % LANES).astype(jnp.bfloat16)


def of_station(groups, values, station, stations):
    templates = groups.shape[0]
    named = jnp.stack([template_at(p, stations, templates, station) for p in range(templates)])
    here = (groups == station)[None] & (lax.iota(jnp.int32, templates)[None] == named[:, None])[:, :, None]
    return jnp.sum(jnp.where(here[..., None], values[None], 0), axis=(1, 2))


def pick_rows(groups, offsets, station, stations, signal):
    templates, _, slots = offsets.shape
    count = signal.shape[0]
    wanted = of_station(groups, offsets + 1, station, stations) - 1
    hot = wanted[..., None] == lax.broadcasted_iota(jnp.int32, (1, 1, count), 2)
    hot = hot.reshape(templates * slots, count).astype(signal.dtype)
    return jnp.dot(hot, signal, preferred_element_type=jnp.float32).astype(signal.dtype)


def shards(signal, waveforms, station_groups, channel_offsets, moveouts):
    templates, touches, slots, length = waveforms.shape
    samples = signal.shape[1]
    parts = lax.axis_size("tmpl")
    stations = lax.axis_size("stn")
    station = lax.axis_index("stn")
    groups = station_groups.T
    half, quarter = templates // 2, templates // 4
    if parts == 2:
        swap = [(0, 1), (1, 0)]
        if templates == slots:
            packed = lax.optimization_barrier(jnp.concatenate([channel_offsets, groups[None]], axis=0))
            named, asked = [(x[templates].T, x[:templates]) for x in (packed, lax.ppermute(packed, "tmpl", swap))]
        else:
            named = station_groups, channel_offsets
            asked = [lax.ppermute(x, "tmpl", swap) for x in named]
        own = pick_rows(*named, station, stations, signal)
        asked, own = lax.optimization_barrier((asked, own))
        sent = pick_rows(*asked, station, stations, signal)
        sent, groups = lax.optimization_barrier((sent, groups))
        got = lax.ppermute(sent, "tmpl", swap)

        def pieces(first):
            return (own, first * slots), (got, first * slots)
    else:
        asked = [lax.all_gather(x, "tmpl", axis=0) for x in (station_groups, channel_offsets)]
        sent = jnp.stack([pick_rows(asked[0][i], asked[1][i], station, stations, signal) for i in range(parts)])
        got = lax.all_to_all(sent, "tmpl", split_axis=0, concat_axis=0, tiled=True)
        got = got.transpose(1, 0, 2).reshape(templates * slots, parts * samples)

        def pieces(first):
            return ((got, first * slots),)

    tiles, inv, scalars = make_tiles(groups, moveouts, waveforms, stations)
    band = band_matrix(length)

    def stacks(first, last):
        positions = tuple(range(first, last))
        return make_stacks(positions, scalars, slots, pieces(first), tiles, inv, band, length)

    def across(x, step):
        return lax.ppermute(x, "stn", [(j, j ^ step) for j in range(stations)])

    came = across(stacks(0, half), 1)
    left = stacks(half, half + quarter) + came[:quarter]
    came_left = across(left, 2)
    total = stacks(half + quarter, templates) + came[quarter:] + came_left
    step = 4
    while step < stations:
        middle = total.shape[0] // 2
        total = total[middle:] + across(total[:middle], step)
        step *= 2
    return total.reshape(templates // stations, NT)


def solution(mesh):
    in_specs = (
        P("stn", ("span", "tmpl")),
        P("tmpl", None, None, None),
        P("tmpl", None),
        P("tmpl", None, None),
        P("tmpl", None, None),
    )
    out_specs = P(("tmpl", "stn"), "span")
    return jax.shard_map(shards, mesh=mesh, in_specs=in_specs, out_specs=out_specs, check_vma=False)
```

```python
import functools
import jax
import jax.numpy as jnp
from jax import lax
from jax.experimental import pallas as pl
from jax.experimental.pallas import tpu as pltpu
from jax.sharding import PartitionSpec as P

NT = 3072
LANES = 128
eps_value = 1e-05
KERNEL_VMEM = 24 << 20


def order_of(stations):
    bits = stations.bit_length() - 1
    reverse = lambda m: sum(((m >> b) & 1) << (bits - 1 - b) for b in range(bits))
    return sorted(range(stations), key=reverse, reverse=True)


def template_at(position, stations, templates, station):
    own_rows = templates // stations
    entry = order_of(stations)[position // own_rows]
    return (entry ^ station) * own_rows + position % own_rows


def toeplitz_kernel(
    slots, length, span, stations, groups_ref, shift_ref, waves_ref, tiles_ref, inv_ref, scalar_ref, padded, flipped
):
    templates = waves_ref.shape[0]
    taps = span // LANES
    rows = templates * slots
    station = lax.axis_index("stn")
    padded[...] = jnp.zeros_like(padded)
    groups = groups_ref[...]
    number = lax.broadcasted_iota(jnp.int32, groups.shape, 0)
    column = lax.broadcasted_iota(jnp.int32, groups.shape, 1)
    for p in range(templates):
        k = template_at(p, stations, templates, station)
        touch = jnp.sum(jnp.where((column == k) & (groups == station), number, 0))
        scalar_ref[p : p + 1, :] = shift_ref[k, pl.ds(touch, 1), :]
        waves = waves_ref[k, touch].astype(jnp.float32)
        power = jnp.sum(waves * waves, axis=1, keepdims=True) / length
        inv = 1.0 / (length * jnp.sqrt(power + eps_value))
        inv_ref[p * slots : (p + 1) * slots, :] = jnp.broadcast_to(inv, (slots, LANES))
        padded[p * slots : (p + 1) * slots, 0:length] = waves
    down = lax.broadcasted_iota(jnp.int32, (LANES, LANES), 0)
    along = lax.broadcasted_iota(jnp.int32, (LANES, LANES), 1)
    exchange = (down + along == LANES - 1).astype(jnp.bfloat16)
    for q in range(taps):
        block = padded[:, (taps - 1 - q) * LANES : (taps - q) * LANES].astype(jnp.bfloat16)
        flipped[:, q * LANES : (q + 1) * LANES] = jnp.dot(block, exchange, preferred_element_type=jnp.float32)
    for row in range(rows):
        turned = jnp.broadcast_to(flipped[row : row + 1, :], (LANES, span))
        turned = pltpu.roll(turned, 1, 1, stride=1, stride_axis=0).astype(jnp.bfloat16)
        for o in range(taps):
            lanes = (taps - o) % taps * LANES
            tiles_ref[row, o * LANES : (o + 1) * LANES, :] = turned[:, lanes : lanes + LANES]


def make_tiles(groups, shifts, waves, stations):
    templates, _, slots, length = waves.shape
    span = LANES * (-(-(LANES + length - 1) // LANES))
    rows = templates * slots
    vmem = pl.BlockSpec(memory_space=pltpu.VMEM)
    return pl.pallas_call(
        functools.partial(toeplitz_kernel, slots, length, span, stations),
        out_shape=(
            jax.ShapeDtypeStruct((rows, span, LANES), jnp.bfloat16),
            jax.ShapeDtypeStruct((rows, LANES), jnp.float32),
            jax.ShapeDtypeStruct((templates, slots), jnp.int32),
        ),
        in_specs=[vmem] * 3,
        out_specs=(vmem, vmem, vmem),
        scratch_shapes=[pltpu.VMEM((rows, span), jnp.float32), pltpu.VMEM((rows, span), jnp.float32)],
        name="toeplitz",
        cost_estimate=pl.CostEstimate(flops=10000000, bytes_accessed=9000000, transcendentals=0),
        compiler_params=pltpu.CompilerParams(vmem_limit_bytes=KERNEL_VMEM),
    )(groups, shifts, waves)


def stack_kernel(slots, length, blocks, positions, starts, scalar_ref, *refs):
    pieces = len(starts)
    piece_refs, refs = refs[:pieces], refs[pieces:]
    tiles_ref, inv_ref, band_ref, out_ref, raw, rolled, aligned, sums, whole = refs
    taps = tiles_ref.shape[1] // LANES
    rows = len(positions) * slots
    pitch = raw.shape[0] // rows
    wide = aligned.shape[0] // rows
    for i, piece in enumerate(piece_refs):
        start = 0
        if pieces == 2:
            me = lax.axis_index("tmpl")
            start = (me if i == 0 else 1 - me) * (piece.shape[1] // LANES)
        for a in range(piece.shape[1] // LANES):
            for r in range(0, rows, 8):
                first = starts[i] + r
                part = piece[first : first + 8, a * LANES : (a + 1) * LANES].astype(jnp.float32)
                raw[pl.ds(r * pitch + start + a, 8, stride=pitch), :] = part
    lane = lax.broadcasted_iota(jnp.int32, (wide, LANES), 1)

    scalars = scalar_ref[...]
    for i, position in enumerate(positions):
        for s in range(slots):
            row = i * slots + s
            shift = scalars[position, s]
            block = shift >> 7
            fine = shift & (LANES - 1)
            turned = pltpu.roll(raw[pl.ds(row * pitch + block, wide), :], LANES - fine, 1)
            rolled[row, 0:wide, :] = turned
            value = jnp.where(lane < LANES - fine, turned, rolled[row, pl.ds(1, wide), :])
            aligned[row * wide : (row + 1) * wide, :] = value
    value = aligned[...]
    square = value * value
    high = square.astype(jnp.bfloat16)
    low = (square - high.astype(jnp.float32)).astype(jnp.bfloat16)
    part = jnp.dot(jnp.concatenate([high, low], axis=1), band_ref[...], preferred_element_type=jnp.float32)
    sums[...] = part
    whole[...] = jnp.broadcast_to(part[:, 0:1], whole.shape)

    full, rest = length // LANES, length % LANES
    ahead = lax.broadcasted_iota(jnp.int32, (blocks, LANES), 1) < LANES - rest

    def energy_of(row):
        first = row * wide
        energy = sums[pl.ds(first, blocks), 0:LANES]
        for o in range(1, full):
            energy = energy + whole[pl.ds(first + o, blocks), :]
        near = sums[pl.ds(first + full, blocks), LANES : 2 * LANES]
        far = sums[pl.ds(first + full + 1, blocks), LANES : 2 * LANES]
        return energy + jnp.where(ahead, near, whole[pl.ds(first + full, blocks), :] + far)

    for i, position in enumerate(positions):
        total = jnp.zeros((blocks, LANES), jnp.float32)
        for s in range(0, slots, 2):
            row = i * slots + s
            window = jnp.concatenate(
                [
                    jnp.concatenate([aligned[pl.ds((row + h) * wide + o, blocks), :] for h in range(2)], axis=0)
                    for o in range(taps)
                ],
                axis=1,
            ).astype(jnp.bfloat16)
            first = position * slots + s
            tiles = jnp.concatenate([tiles_ref[first], tiles_ref[first + 1]], axis=1)
            correl = jnp.dot(window, tiles, preferred_element_type=jnp.float32)
            for h in range(2):
                weight = inv_ref[pl.ds(first + h, 1), :]
                scale = lax.rsqrt(energy_of(row + h) / length + eps_value) * weight
                total = total + correl[h * blocks : (h + 1) * blocks, h * LANES : (h + 1) * LANES] * scale
        out_ref[i] = total


def make_stacks(positions, scalars, slots, pieces, tiles, inv, band, length):
    taps = tiles.shape[1] // LANES
    rows = len(positions) * slots
    blocks = NT // LANES
    wide = 8 * (-(-(blocks + taps - 1) // 8))
    depth = sum(p.shape[1] for p, _ in pieces) // LANES
    pitch = 8 * (-(-(depth + wide - blocks) // 8)) + 1
    vmem = pl.BlockSpec(memory_space=pltpu.VMEM)
    return pl.pallas_call(
        functools.partial(stack_kernel, slots, length, blocks, positions, tuple(first for _, first in pieces)),
        out_shape=jax.ShapeDtypeStruct((len(positions), blocks, LANES), jnp.float32),
        in_specs=[vmem] * (len(pieces) + 4),
        out_specs=vmem,
        scratch_shapes=[
            pltpu.VMEM((rows * pitch, LANES), jnp.float32),
            pltpu.VMEM((rows, wide + 8, LANES), jnp.float32),
            pltpu.VMEM((rows * wide, LANES), jnp.float32),
            pltpu.VMEM((rows * wide, 2 * LANES), jnp.float32),
            pltpu.VMEM((rows * wide, LANES), jnp.float32),
        ],
        name="stack",
        cost_estimate=pl.CostEstimate(
            flops=50000000 * len(positions), bytes_accessed=1000000 * len(positions), transcendentals=0
        ),
        compiler_params=pltpu.CompilerParams(vmem_limit_bytes=KERNEL_VMEM),
    )(scalars, *[p for p, _ in pieces], tiles, inv, band)


def band_matrix(length):
    c = lax.broadcasted_iota(jnp.int32, (2 * LANES, 2 * LANES), 0) % LANES
    b = lax.broadcasted_iota(jnp.int32, (2 * LANES, 2 * LANES), 1)
    return jnp.where(b < LANES, c >= b, c < (b + length) % LANES).astype(jnp.bfloat16)


def of_station(groups, values, station, stations):
    templates = groups.shape[0]
    named = jnp.stack([template_at(p, stations, templates, station) for p in range(templates)])
    here = (groups == station)[None] & (lax.iota(jnp.int32, templates)[None] == named[:, None])[:, :, None]
    return jnp.sum(jnp.where(here[..., None], values[None], 0), axis=(1, 2))


def pick_rows(groups, offsets, station, stations, signal):
    templates, _, slots = offsets.shape
    count = signal.shape[0]
    wanted = of_station(groups, offsets + 1, station, stations)
    hot = wanted[..., None] == 1 + lax.broadcasted_iota(jnp.int32, (1, 1, count), 2)
    hot = hot.reshape(templates * slots, count).astype(signal.dtype)
    return jnp.dot(hot, signal, preferred_element_type=jnp.float32).astype(signal.dtype)


def shards(signal, waveforms, station_groups, channel_offsets, moveouts):
    templates, _, slots, length = waveforms.shape
    samples = signal.shape[1]
    parts = lax.axis_size("tmpl")
    stations = lax.axis_size("stn")
    station = lax.axis_index("stn")
    groups = station_groups.T
    half, quarter = templates // 2, templates // 4
    if parts == 2:
        swap = [(0, 1), (1, 0)]
        if templates == slots:
            packed = lax.optimization_barrier(jnp.concatenate([channel_offsets, groups[None]], axis=0))
            named, asked = [(x[templates].T, x[:templates]) for x in (packed, lax.ppermute(packed, "tmpl", swap))]
        else:
            named = station_groups, channel_offsets
            asked = [lax.ppermute(x, "tmpl", swap) for x in named]
        own = pick_rows(*named, station, stations, signal)
        asked, own = lax.optimization_barrier((asked, own))
        sent = pick_rows(*asked, station, stations, signal)
        sent, groups = lax.optimization_barrier((sent, groups))
        got = lax.ppermute(sent, "tmpl", swap)

        def pieces(first):
            return (own, first * slots), (got, first * slots)
    else:
        asked = [lax.all_gather(x, "tmpl", axis=0) for x in (station_groups, channel_offsets)]
        sent = jnp.stack([pick_rows(asked[0][i], asked[1][i], station, stations, signal) for i in range(parts)])
        got = lax.all_to_all(sent, "tmpl", split_axis=0, concat_axis=0, tiled=True)
        got = got.transpose(1, 0, 2).reshape(templates * slots, parts * samples)

        def pieces(first):
            return ((got, first * slots),)

    tiles, inv, scalars = make_tiles(groups, moveouts, waveforms, stations)
    band = band_matrix(length)

    def stacks(first, last, inv):
        positions = tuple(range(first, last))
        return make_stacks(positions, scalars, slots, pieces(first), tiles, inv, band, length)

    def across(x, step):
        return lax.ppermute(x, "stn", [(j, j ^ step) for j in range(stations)])

    came = across(stacks(0, quarter, inv), 1)
    left = stacks(half, half + quarter, inv) + came
    came_left = across(left, 2)
    away = stacks(quarter, half, inv)
    came = across(away, 1)
    kept = stacks(half + quarter, templates, inv)
    total = kept + came + came_left
    step = 4
    while step < stations:
        middle = total.shape[0] // 2
        total = total[middle:] + across(total[:middle], step)
        step *= 2
    return total.reshape(templates // stations, NT)


def solution(mesh):
    in_specs = (
        P("stn", ("span", "tmpl")),
        P("tmpl", None, None, None),
        P("tmpl", None),
        P("tmpl", None, None),
        P("tmpl", None, None),
    )
    out_specs = P(("tmpl", "stn"), "span")
    return jax.shard_map(shards, mesh=mesh, in_specs=in_specs, out_specs=out_specs, check_vma=False)
```

```python
import functools
import jax
import jax.numpy as jnp
from jax import lax
from jax.experimental import pallas as pl
from jax.experimental.pallas import tpu as pltpu
from jax.sharding import PartitionSpec as P

NT = 3072
LANES = 128
eps_value = 1e-05
KERNEL_VMEM = 24 << 20


def order_of(stations):
    bits = stations.bit_length() - 1
    reverse = lambda m: sum(((m >> b) & 1) << (bits - 1 - b) for b in range(bits))
    return sorted(range(stations), key=reverse, reverse=True)


def template_at(position, stations, templates, station):
    own_rows = templates // stations
    entry = order_of(stations)[position // own_rows]
    return (entry ^ station) * own_rows + position % own_rows


def toeplitz_kernel(
    slots, length, span, stations, groups_ref, shift_ref, waves_ref, tiles_ref, inv_ref, scalar_ref, padded, flipped
):
    templates = waves_ref.shape[0]
    taps = span // LANES
    rows = templates * slots
    station = lax.axis_index("stn")
    padded[...] = jnp.zeros_like(padded)
    groups = groups_ref[...]
    number = lax.broadcasted_iota(jnp.int32, groups.shape, 0)
    column = lax.broadcasted_iota(jnp.int32, groups.shape, 1)
    for p in range(templates):
        k = template_at(p, stations, templates, station)
        touch = jnp.sum(jnp.where((column == k) & (groups == station), number, 0))
        scalar_ref[p : p + 1, :] = shift_ref[k, pl.ds(touch, 1), :]
        waves = waves_ref[k, touch].astype(jnp.float32)
        power = jnp.sum(waves * waves, axis=1, keepdims=True) / length
        inv = 1.0 / (length * jnp.sqrt(power + eps_value))
        inv_ref[p * slots : (p + 1) * slots, :] = jnp.broadcast_to(inv, (slots, LANES))
        padded[p * slots : (p + 1) * slots, 0:length] = waves
    down = lax.broadcasted_iota(jnp.int32, (LANES, LANES), 0)
    along = lax.broadcasted_iota(jnp.int32, (LANES, LANES), 1)
    exchange = (down + along == LANES - 1).astype(jnp.bfloat16)
    for q in range(taps):
        block = padded[:, (taps - 1 - q) * LANES : (taps - q) * LANES].astype(jnp.bfloat16)
        flipped[:, q * LANES : (q + 1) * LANES] = jnp.dot(block, exchange, preferred_element_type=jnp.float32)
    for row in range(rows):
        turned = jnp.broadcast_to(flipped[row : row + 1, :], (LANES, span))
        turned = pltpu.roll(turned, 1, 1, stride=1, stride_axis=0).astype(jnp.bfloat16)
        for o in range(taps):
            lanes = (taps - o) % taps * LANES
            tiles_ref[row, o * LANES : (o + 1) * LANES, :] = turned[:, lanes : lanes + LANES]


def make_tiles(groups, shifts, waves, stations):
    templates, _, slots, length = waves.shape
    span = LANES * (-(-(LANES + length - 1) // LANES))
    rows = templates * slots
    vmem = pl.BlockSpec(memory_space=pltpu.VMEM)
    return pl.pallas_call(
        functools.partial(toeplitz_kernel, slots, length, span, stations),
        out_shape=(
            jax.ShapeDtypeStruct((rows, span, LANES), jnp.bfloat16),
            jax.ShapeDtypeStruct((rows, LANES), jnp.float32),
            jax.ShapeDtypeStruct((templates, slots), jnp.int32),
        ),
        in_specs=[vmem] * 3,
        out_specs=(vmem, vmem, vmem),
        scratch_shapes=[pltpu.VMEM((rows, span), jnp.float32), pltpu.VMEM((rows, span), jnp.float32)],
        name="toeplitz",
        cost_estimate=pl.CostEstimate(flops=10000000, bytes_accessed=9000000, transcendentals=0),
        compiler_params=pltpu.CompilerParams(vmem_limit_bytes=KERNEL_VMEM),
    )(groups, shifts, waves)


def stack_kernel(slots, length, blocks, positions, starts, scalar_ref, *refs):
    pieces = len(starts)
    piece_refs, refs = refs[:pieces], refs[pieces:]
    tiles_ref, inv_ref, band_ref, out_ref, raw, rolled, aligned, sums, whole = refs
    taps = tiles_ref.shape[1] // LANES
    rows = len(positions) * slots
    pitch = raw.shape[0] // (rows + 1)
    wide = aligned.shape[0] // rows
    for i, piece in enumerate(piece_refs):
        start = 0
        if pieces == 2:
            me = lax.axis_index("tmpl")
            start = (me if i == 0 else 1 - me) * (piece.shape[1] // LANES)
        for a in range(piece.shape[1] // LANES):
            for r in range(0, rows, 8):
                first = starts[i] + r
                part = piece[first : first + 8, a * LANES : (a + 1) * LANES].astype(jnp.float32)
                raw[pl.ds(r * pitch + start + a, 8, stride=pitch), :] = part
    lane = lax.broadcasted_iota(jnp.int32, (wide, LANES), 1)

    scalars = scalar_ref[...]
    for i, position in enumerate(positions):
        for s in range(slots):
            row = i * slots + s
            shift = scalars[position, s]
            block = shift >> 7
            fine = shift & (LANES - 1)
            turned = pltpu.roll(raw[pl.ds(row * pitch + block, wide), :], LANES - fine, 1)
            rolled[row, 0:wide, :] = turned
            value = jnp.where(lane < LANES - fine, turned, rolled[row, pl.ds(1, wide), :])
            aligned[row * wide : (row + 1) * wide, :] = value
    value = aligned[...]
    square = value * value
    high = square.astype(jnp.bfloat16)
    low = (square - high.astype(jnp.float32)).astype(jnp.bfloat16)
    part = jnp.dot(jnp.concatenate([high, low], axis=1), band_ref[...], preferred_element_type=jnp.float32)
    sums[...] = part
    whole[...] = jnp.broadcast_to(part[:, 0:1], whole.shape)

    full, rest = length // LANES, length % LANES
    ahead = lax.broadcasted_iota(jnp.int32, (blocks, LANES), 1) < LANES - rest

    def energy_of(row):
        first = row * wide
        energy = sums[pl.ds(first, blocks), 0:LANES]
        for o in range(1, full):
            energy = energy + whole[pl.ds(first + o, blocks), :]
        near = sums[pl.ds(first + full, blocks), LANES : 2 * LANES]
        far = sums[pl.ds(first + full + 1, blocks), LANES : 2 * LANES]
        return energy + jnp.where(ahead, near, whole[pl.ds(first + full, blocks), :] + far)

    for i, position in enumerate(positions):
        total = jnp.zeros((blocks, LANES), jnp.float32)
        for s in range(0, slots, 2):
            row = i * slots + s
            window = jnp.concatenate(
                [
                    jnp.concatenate([aligned[pl.ds((row + h) * wide + o, blocks), :] for h in range(2)], axis=0)
                    for o in range(taps)
                ],
                axis=1,
            ).astype(jnp.bfloat16)
            first = position * slots + s
            tiles = jnp.concatenate([tiles_ref[first], tiles_ref[first + 1]], axis=1)
            correl = jnp.dot(window, tiles, preferred_element_type=jnp.float32)
            for h in range(2):
                weight = inv_ref[pl.ds(first + h, 1), :]
                scale = lax.rsqrt(energy_of(row + h) / length + eps_value) * weight
                total = total + correl[h * blocks : (h + 1) * blocks, h * LANES : (h + 1) * LANES] * scale
        out_ref[i] = total


def make_stacks(positions, scalars, slots, pieces, tiles, inv, band, length):
    taps = tiles.shape[1] // LANES
    rows = len(positions) * slots
    blocks = NT // LANES
    wide = 8 * (-(-(blocks + taps - 1) // 8))
    depth = sum(p.shape[1] for p, _ in pieces) // LANES
    pitch = 8 * (-(-(depth + wide - blocks) // 8)) + 1
    vmem = pl.BlockSpec(memory_space=pltpu.VMEM)
    return pl.pallas_call(
        functools.partial(stack_kernel, slots, length, blocks, positions, tuple(first for _, first in pieces)),
        out_shape=jax.ShapeDtypeStruct((len(positions), blocks, LANES), jnp.float32),
        in_specs=[vmem] * (len(pieces) + 4),
        out_specs=vmem,
        scratch_shapes=[
            pltpu.VMEM(((rows + 1) * pitch, LANES), jnp.float32),
            pltpu.VMEM((rows, wide + 8, LANES), jnp.float32),
            pltpu.VMEM((rows * wide, LANES), jnp.float32),
            pltpu.VMEM((rows * wide, 2 * LANES), jnp.float32),
            pltpu.VMEM((rows * wide, LANES), jnp.float32),
        ],
        name="stack",
        cost_estimate=pl.CostEstimate(
            flops=50000000 * len(positions), bytes_accessed=1000000 * len(positions), transcendentals=0
        ),
        compiler_params=pltpu.CompilerParams(vmem_limit_bytes=KERNEL_VMEM),
    )(scalars, *[p for p, _ in pieces], tiles, inv, band)


def band_matrix(length):
    c = lax.broadcasted_iota(jnp.int32, (2 * LANES, 2 * LANES), 0) % LANES
    b = lax.broadcasted_iota(jnp.int32, (2 * LANES, 2 * LANES), 1)
    return jnp.where(b < LANES, c >= b, c < (b + length) % LANES).astype(jnp.bfloat16)


def of_station(groups, values, station, stations):
    templates = groups.shape[0]
    named = jnp.stack([template_at(p, stations, templates, station) for p in range(templates)])
    here = (groups == station)[None] & (lax.iota(jnp.int32, templates)[None] == named[:, None])[:, :, None]
    return jnp.sum(jnp.where(here[..., None], values[None], 0), axis=(1, 2))


def pick_rows(groups, offsets, station, stations, signal):
    templates, _, slots = offsets.shape
    count = signal.shape[0]
    wanted = of_station(groups, offsets + 1, station, stations)
    hot = wanted[..., None] == 1 + lax.broadcasted_iota(jnp.int32, (1, 1, count), 2)
    rows = jnp.dot(hot.astype(signal.dtype), signal, preferred_element_type=jnp.float32).astype(signal.dtype)
    return rows.reshape(templates * slots, signal.shape[1])


def shards(signal, waveforms, station_groups, channel_offsets, moveouts):
    templates, _, slots, length = waveforms.shape
    samples = signal.shape[1]
    parts = lax.axis_size("tmpl")
    stations = lax.axis_size("stn")
    station = lax.axis_index("stn")
    groups = station_groups.T
    half, quarter = templates // 2, templates // 4
    if parts == 2:
        swap = [(0, 1), (1, 0)]
        if templates == slots:
            packed = lax.optimization_barrier(jnp.concatenate([channel_offsets, groups[None]], axis=0))
            named, asked = [(x[templates].T, x[:templates]) for x in (packed, lax.ppermute(packed, "tmpl", swap))]
        else:
            named = station_groups, channel_offsets
            asked = [lax.ppermute(x, "tmpl", swap) for x in named]
        own = pick_rows(*named, station, stations, signal)
        asked, own = lax.optimization_barrier((asked, own))
        sent = pick_rows(*asked, station, stations, signal)
        sent, groups = lax.optimization_barrier((sent, groups))
        got = lax.ppermute(sent, "tmpl", swap)

        def pieces(first):
            return (own, first * slots), (got, first * slots)
    else:
        asked = [lax.all_gather(x, "tmpl", axis=0) for x in (station_groups, channel_offsets)]
        sent = jnp.stack([pick_rows(asked[0][i], asked[1][i], station, stations, signal) for i in range(parts)])
        got = lax.all_to_all(sent, "tmpl", split_axis=0, concat_axis=0, tiled=True)
        got = got.transpose(1, 0, 2).reshape(templates * slots, parts * samples)

        def pieces(first):
            return ((got, first * slots),)

    tiles, inv, scalars = make_tiles(groups, moveouts, waveforms, stations)
    band = band_matrix(length)

    def stacks(first, last, inv):
        positions = tuple(range(first, last))
        return make_stacks(positions, scalars, slots, pieces(first), tiles, inv, band, length)

    def across(x, step):
        return lax.ppermute(x, "stn", [(j, j ^ step) for j in range(stations)])

    came = across(stacks(0, quarter, inv), 1)
    left = stacks(half, half + quarter, inv) + came
    came_left = across(left, 2)
    away = stacks(quarter, half, inv)
    came = across(away, 1)
    kept = stacks(half + quarter, templates, inv)
    total = kept + came + came_left
    step = 4
    while step < stations:
        middle = total.shape[0] // 2
        total = total[middle:] + across(total[:middle], step)
        step *= 2
    return total.reshape(templates // stations, NT)


def solution(mesh):
    in_specs = (
        P("stn", ("span", "tmpl")),
        P("tmpl", None, None, None),
        P("tmpl", None),
        P("tmpl", None, None),
        P("tmpl", None, None),
    )
    out_specs = P(("tmpl", "stn"), "span")
    return jax.shard_map(shards, mesh=mesh, in_specs=in_specs, out_specs=out_specs, check_vma=False)
```
